32 devices in a mesh: col: 4 (over y, core), row: 8 (over z, x).
Axes of the slice: x: 2, y: 2, z: 4, core: 2. Of those that a mesh axis runs over, the one named last changes fastest.
Arguments:
- tokens: bfloat16 [2048, 2880], P('row'), may hold values from -6 to 6
- moe_gain: bfloat16 [2880], replicated, may hold values from 0.5 to 1.5
- route_ids: int32 [2048, 4], P('row'), may hold values from 0 to 63, all different within a row; in each aligned block of 256 rows (0 to 255, 256 to 511, ...) at most 24 rows name the same one
- route_weight: float32 [2048, 4], P('row'), may hold values from 0.1 to 1
- w_gate: bfloat16 [64, 2880, 2880], P('row', None, 'col'), may hold values from -0.109375 to 0.109375
- w_up: bfloat16 [64, 2880, 2880], P('row', None, 'col'), may hold values from -0.109375 to 0.109375
- w_down: bfloat16 [64, 2880, 2880], P('row', 'col'), may hold values from -0.109375 to 0.109375
- next_gain: bfloat16 [2880], replicated, may hold values from 0.5 to 1.5
- next_gate: bfloat16 [2880, 128], P(None, 'col'), may hold values from -2 to 2
- next_ids: int32 [2048, 4], P('row'), may hold values from 0 to 127, all different within a row
Outputs:
- mixed: bfloat16 [2048, 2880], P('row', 'col')
- next_logprob: float32 [2048, 4], P('row')
The draws below stay inside these ranges and needn't reach their ends.
Inputs may be any that keep to these rules, and one draw needn't show every extreme that they name: `route_ids`: among the 256 tokens of one index of row, no expert is picked more than 24 times, a bound that some block reaches; a token's picks differ. `next_ids`: A token's picks differ.
All inputs are finite; a program needn't handle non-finite values.
Results may differ from the reference program's by a relative error of at most 0.0095.
Values may be sent and summed in bfloat16 or wider, within the bound.
A program may use at most 256 MiB of HBM per device.

```python
import math
import jax
import jax.numpy as jnp
import numpy as np
from jax import lax

D = 2880
FF = 2880
EXPERTS = 64
NEXT_EXPERTS = 128
TOP = 4
TOK_ROW = 256
CAP = 24
TOKENS = 2048
N_COL = 4
N_ROW = 8


def joint_draw(key):
    keys = jax.random.split(jax.random.fold_in(key, 7), 3)
    tokens = jax.random.truncated_normal(keys[0], -6.0, 6.0, (TOKENS, D), jnp.float32)
    column_scale = jnp.exp(jax.random.uniform(keys[1], (NEXT_EXPERTS,), jnp.float32, 0.0, math.log(10.0)))
    router = jax.random.truncated_normal(keys[2], -4.0, 4.0, (D, NEXT_EXPERTS), jnp.float32)
    router = router * column_scale[None, :] / math.sqrt(D)
    return (tokens, router)


def draw_tokens(key, part):
    return joint_draw(key)[0].astype(jnp.bfloat16)


def draw_next_gate(key, part):
    return jnp.clip(joint_draw(key)[1], -2.0, 2.0).astype(jnp.bfloat16)


def shard_levels(own_key, dims, cuts, smallest, high):
    gain, own = 1.0, jax.random.fold_in(own_key, 6)
    for position, blocks in cuts:
        heights = jnp.exp(jax.random.uniform(jax.random.fold_in(own, position), (blocks,), jnp.float32, smallest / len(cuts), high / len(cuts)))
        gain = gain * jnp.repeat(heights, dims[position] // blocks).reshape([-1 if axis == position else 1 for axis in range(len(dims))])
    return gain


def different_ones(rng, rows, count, top, lift):
    ranking = jax.random.permutation(jax.random.fold_in(rng, 1), count)
    boost = ranking
    for power in range(3):
        boost = boost * boost // count
    boost = boost * lift // count
    lots = jax.random.randint(jax.random.fold_in(rng, 2), (rows, count), 0, 4096) + boost
    sure = jax.random.permutation(jax.random.fold_in(rng, 3), rows)[jnp.arange(count) % rows]
    lots = jnp.where(jnp.arange(rows)[:, None] == sure[None, :], 1 << 14, lots)
    merit = lots * count + jnp.arange(count)
    return lax.top_k(merit.astype(jnp.int32), top)[1].astype(jnp.int32)


def assign_block(stream_key, own, number, rows, count, top, limit, skew):
    sequence = jax.random.permutation(stream_key, count)
    packed, common = portions_of(count, rows * top, limit, skew, True), portions_of(count, rows * top, limit, skew, False)
    places = jnp.arange(count)

    def named(tallies, turn):
        used = int((tallies > 0).sum())
        fixed = max(1, used // 4)
        passed = fixed + (places - fixed + turn * (used - fixed)) % max(1, count - fixed)
        return jnp.zeros((count,), jnp.int32).at[sequence[jnp.where(places < fixed, places, passed)]].set(jnp.asarray(tallies, jnp.int32))

    tallies = jnp.where(number % 4 == 0, named(packed, number // 4), named(common, number - number // 4 - 1))
    mixed = jax.random.permutation(jax.random.fold_in(own, 3), count)
    donor, receiver = mixed[0:count // 2 * 2:2], mixed[1:count // 2 * 2:2]
    room = jnp.minimum(tallies[donor] - 1, limit - tallies[receiver]) // 2
    room = jnp.where((donor == sequence[0]) | (receiver == sequence[0]) | (tallies[receiver] == 0), 0, jnp.maximum(room, 0))
    passed = jax.random.randint(jax.random.fold_in(own, 4), (count // 2,), 0, 1 << 20) % (room + 1)
    tallies = tallies.at[donor].add(-passed).at[receiver].add(passed)
    labels = jnp.searchsorted(jnp.cumsum(tallies), jnp.arange(rows * top), side="right").astype(jnp.int32)
    grid = labels.reshape(top, rows).T
    grid = grid[jax.random.permutation(jax.random.fold_in(own, 1), rows)]
    turn = jax.random.randint(jax.random.fold_in(own, 2), (rows, 1), 0, top)
    return jnp.take_along_axis(grid, (jnp.arange(top)[None, :] + turn) % top, axis=1)


def portions_of(amount, total, bound, lean, full):
    weights = [(1 << 20) // math.isqrt(grade ** lean) + 1 for grade in range(1, amount + 1)]
    largest = bound if full else min(bound, max(-(-total // amount), total * weights[0] // sum(weights)))
    least = 1 if total - largest >= amount - 1 else 0
    counts, rest = [largest] + [least] * (amount - 1), total - largest - least * (amount - 1)
    while rest > 0:
        free = [i for i in range(1, amount) if counts[i] < largest] or [i for i in range(1, amount) if counts[i] < bound]
        mass, budget = sum([weights[i] for i in free]), rest
        for i in free:
            addition = min(bound - counts[i], max(1, budget * weights[i] // mass), rest)
            counts[i] = counts[i] + addition
            rest = rest - addition
    return np.array(counts)


def bell_draw(own_key, dims, scale, most, cuts=(), held_as=jnp.bfloat16):
    loudness = shard_levels(own_key, dims, cuts, -0.22, 0.18) if cuts else 1.0
    entries = jax.random.normal(own_key, dims, jnp.float32) * scale * loudness
    return jnp.minimum(jnp.maximum(entries, -most), most).astype(held_as)


def setup_inputs(seed: int = 0) -> dict:
    streams_of = jax.random.split(jax.random.key(seed), 11)
    tokens = draw_tokens(jax.random.fold_in(streams_of[10], 71), 0)
    moe_gain = jnp.clip(1.0 + 0.1 * jax.random.normal(streams_of[1], (D,), jnp.float32), 0.5, 1.5).astype(jnp.bfloat16)
    route_ids_keys = jax.random.split(jax.random.fold_in(streams_of[2], 1), TOKENS // TOK_ROW)
    route_ids_turns = jax.random.permutation(jax.random.fold_in(streams_of[2], 3), TOKENS // TOK_ROW)
    route_ids = jax.vmap(lambda own, number: assign_block(jax.random.fold_in(streams_of[2], 2), own, number, TOK_ROW, EXPERTS, TOP, CAP, 2))(route_ids_keys, route_ids_turns).reshape((TOKENS, TOP))
    route_weight = jnp.clip(jnp.exp(math.log(1.0) - 2.3025851 * jax.random.uniform(streams_of[3], (TOKENS, TOP), jnp.float32) ** shard_levels(streams_of[3], (TOKENS, TOP), ((0, 8),), -0.2, 0.2)), 0.1, 1.0)
    w_gate = bell_draw(streams_of[4], (EXPERTS, D, FF), D ** -0.5, 0.109375, ((0, 8), (2, 4)))
    w_up = bell_draw(streams_of[5], (EXPERTS, D, FF), D ** -0.5, 0.109375, ((0, 8), (2, 4)))
    w_down = bell_draw(streams_of[6], (EXPERTS, FF, D), FF ** -0.5, 0.109375, ((0, 8), (1, 4)))
    next_gain = jnp.clip(1.0 + 0.1 * jax.random.normal(streams_of[7], (D,), jnp.float32), 0.5, 1.5).astype(jnp.bfloat16)
    next_gate = draw_next_gate(jax.random.fold_in(streams_of[10], 71), 0)
    next_ids = different_ones(streams_of[9], TOKENS, NEXT_EXPERTS, TOP, 256)
    return dict(tokens=tokens, moe_gain=moe_gain, route_ids=route_ids, route_weight=route_weight, w_gate=w_gate, w_up=w_up, w_down=w_down, next_gain=next_gain, next_gate=next_gate, next_ids=next_ids)


def reference(tokens, moe_gain, route_ids, route_weight, w_gate, w_up, w_down, next_gain, next_gate, next_ids):
    floats = tokens.astype(jnp.float32)
    inverse = lax.rsqrt(lax.optimization_barrier(jnp.mean(floats * floats, axis=-1, keepdims=True)) + 1e-05)
    normed = (floats * inverse * moe_gain.astype(jnp.float32)).astype(jnp.bfloat16)
    gated_in = (floats * inverse * next_gain.astype(jnp.float32)).astype(jnp.bfloat16)
    picks = TOK_ROW * TOP
    blocks = route_ids.reshape(N_ROW, picks)
    onehot = (blocks[:, :, None] == jnp.arange(EXPERTS, dtype=jnp.int32)[None, None, :]).astype(jnp.int32)
    slots = (lax.optimization_barrier(jnp.sum(jnp.cumsum(onehot, axis=1) * onehot, axis=2)) - 1).astype(jnp.int32)
    block_index = jnp.broadcast_to(jnp.arange(N_ROW, dtype=jnp.int32)[:, None], (N_ROW, picks))
    token_of = (block_index * TOK_ROW + jnp.arange(picks, dtype=jnp.int32)[None, :] // TOP).astype(jnp.int32)
    table = jnp.full((EXPERTS, N_ROW, CAP), TOKENS, jnp.int32).at[blocks, block_index, slots].set(token_of)
    padded = jnp.concatenate([normed, jnp.zeros((1, D), jnp.bfloat16)], axis=0)

    def one_expert(inputs):
        index, gate_w, up_w, down_w = inputs
        chosen = padded[index.reshape(-1)].astype(jnp.float32)
        gate = jnp.dot(chosen, gate_w.astype(jnp.float32), preferred_element_type=jnp.float32)
        upward = jnp.dot(chosen, up_w.astype(jnp.float32), preferred_element_type=jnp.float32)
        hidden = (jax.nn.silu(gate) * upward).astype(jnp.bfloat16)
        pieces = jnp.einsum('rcf,cfd->crd', hidden.reshape(-1, N_COL, FF // N_COL).astype(jnp.float32), down_w.reshape(N_COL, FF // N_COL, D).astype(jnp.float32))
        pieces = lax.optimization_barrier(pieces.astype(jnp.bfloat16)).astype(jnp.float32)
        return lax.optimization_barrier(jnp.sum(pieces, axis=0)).astype(jnp.bfloat16)
    outputs = lax.map(one_expert, (table, w_gate, w_up, w_down))
    flat_out = outputs.reshape(EXPERTS * N_ROW * CAP, D)
    where = (blocks * (N_ROW * CAP) + block_index * CAP + slots).astype(jnp.int32)
    gathered = flat_out[where.reshape(-1)].astype(jnp.float32).reshape(TOKENS, TOP, D)
    combined = lax.optimization_barrier(jnp.sum(gathered * route_weight[:, :, None], axis=1))
    mixed = (floats + combined).astype(jnp.bfloat16)
    logits = jnp.dot(gated_in, next_gate, preferred_element_type=jnp.float32)
    highest = lax.optimization_barrier(jnp.max(logits, axis=-1))
    total = lax.optimization_barrier(jnp.sum(jnp.exp(logits - highest[:, None]), axis=-1))
    picked = jnp.take_along_axis(logits, next_ids, axis=1)
    next_logprob = picked - highest[:, None] - jnp.log(total)[:, None]
    return (mixed, next_logprob)
```

```python
import functools

import jax
import jax.numpy as jnp
from jax import lax
from jax.experimental import pallas as pl
from jax.experimental.pallas import tpu as pltpu
from jax.sharding import PartitionSpec as P

TOP = 4
CAP = 24


MESH = pl.DeviceIdType.MESH


def ring_place(row, rows):
    return row // 2 + (row % 2) * (rows - 1 - 2 * (row // 2))


def ring_row(place, rows):
    place = (place + 2 * rows) % rows
    far = place // (rows // 2)
    return (1 - far) * 2 * place + far * (2 * (rows - 1 - place) + 1)


def lanes_of(rows):
    half = rows // 2
    found = []
    for distance in range(1, half + 1):
        for way in (0, 1):
            for sub in (0, 1):
                if distance < half or way == sub:
                    found.append((len(found), 1 - 2 * way, sub, distance))
    return found


def remote(src, dst, send, recv, target):
    return pltpu.make_async_remote_copy(
        src_ref=src, dst_ref=dst, send_sem=send, recv_sem=recv, device_id=target, device_id_type=MESH
    )


def greet(rows, cols, all_cols):
    row, col = lax.axis_index("row"), lax.axis_index("col")
    barrier = pltpu.get_barrier_semaphore()
    for step in range(1, rows):
        pl.semaphore_signal(
            barrier, inc=1, device_id={"row": (row + step) % rows}, device_id_type=MESH
        )
    others = range(1, cols) if all_cols else ()
    for step in others:
        pl.semaphore_signal(
            barrier, inc=1, device_id={"col": (col + step) % cols}, device_id_type=MESH
        )
    pl.semaphore_wait(barrier, rows - 1 + len(others))


def gather_kernel(
    rows, cols, x_ref, info_ref, out_ref, all_ref, ring_s, ring_r, pair_s, pair_r, info_s, info_r, own_s
):
    row, col = lax.axis_index("row"), lax.axis_index("col")
    core = col % 2
    mate = {"col": col + 1 - 2 * core}
    place = ring_place(row, rows)
    tok = x_ref.shape[0]
    quarter = tok // 4
    greet(rows, cols, True)
    infos = []
    for step in range(1, rows):
        copy = remote(
            info_ref, all_ref.at[row], info_s.at[step - 1], info_r.at[step - 1],
            {"row": (row + step) % rows},
        )
        copy.start()
        infos.append(copy)
    own = pltpu.make_async_copy(x_ref, out_ref.at[row], own_s)

    def span(sub):
        return pl.ds(pl.multiple_of(core * 2 * quarter, quarter) + sub * quarter, quarter)

    lanes = lanes_of(rows)
    where = {(way, sub, far): index for index, way, sub, far in lanes}
    sends = {}

    def send(way, sub, far):
        index = where[way, sub, far]
        block = ring_row(place - way * (far - 1), rows)
        src = x_ref.at[span(sub)] if far == 1 else out_ref.at[block, span(sub)]
        copy = remote(
            src, out_ref.at[block, span(sub)], ring_s.at[index], ring_r.at[index],
            {"row": ring_row(place + way, rows)},
        )
        copy.start()
        sends[index] = copy

    for index, way, sub, far in lanes:
        if far == 1:
            send(way, sub, far)
    own.start()
    pairs = []
    for index, way, sub, far in lanes:
        sends[index].wait_recv()
        if (way, sub, far + 1) in where:
            send(way, sub, far + 1)
        block = ring_row(place - way * far, rows)
        piece = out_ref.at[block, span(sub)]
        copy = remote(piece, piece, pair_s.at[index], pair_r.at[index], mate)
        copy.start()
        pairs.append(copy)
    all_ref[row] = info_ref[...]
    for copy in infos:
        copy.wait()
    own.wait()
    for index, *_ in lanes:
        sends[index].wait_send()
    for copy in pairs:
        copy.wait()


def gather(x, info):
    rows, cols = lax.axis_size("row"), lax.axis_size("col")
    count = len(lanes_of(rows))
    dma = pltpu.SemaphoreType.DMA
    return pl.pallas_call(
        functools.partial(gather_kernel, rows, cols),
        out_shape=(
            jax.ShapeDtypeStruct((rows,) + x.shape, x.dtype),
            jax.ShapeDtypeStruct((rows,) + info.shape, info.dtype),
        ),
        in_specs=[pl.BlockSpec(memory_space=pltpu.VMEM)] * 2,
        out_specs=(pl.BlockSpec(memory_space=pl.ANY), pl.BlockSpec(memory_space=pltpu.VMEM)),
        scratch_shapes=[
            dma((count,)), dma((count,)), dma((count,)), dma((count,)),
            dma((rows - 1,)), dma((rows - 1,)), dma(()),
        ],
        compiler_params=pltpu.CompilerParams(collective_id=0, has_side_effects=True),
        name="gather",
    )(x, info)


def reduce_kernel(
    rows, cols, x_ref, out_ref, mate_buf, got, made, last, parts,
    pair_s, pair_r, ring_s, ring_r, col_s, col_r,
):
    row, col = lax.axis_index("row"), lax.axis_index("col")
    core = col % 2
    place = ring_place(row, rows)
    tok, dim = x_ref.shape[1:]
    quarter = tok // 4
    part = dim // cols
    strip = 16
    greet(rows, cols, True)
    lanes = lanes_of(rows)
    where = {(way, sub, far): index for index, way, sub, far in lanes}
    wanted = list(reversed(lanes)) + [(len(lanes), 1, 0, 0), (len(lanes) + 1, 1, 1, 0)]

    def start_of(owner, sub):
        return pl.multiple_of(owner * 2 * quarter, quarter) + sub * quarter

    pairs = {}
    for index, way, sub, far in wanted:
        block = ring_row(place + way * far, rows)
        copy = remote(
            x_ref.at[block, pl.ds(start_of(1 - core, sub), quarter)], mate_buf.at[index],
            pair_s.at[index], pair_r.at[index], {"col": col + 1 - 2 * core},
        )
        copy.start()
        pairs[index] = copy
    sends = {}

    def total(index, way, sub, far, store):
        pairs[index].wait_recv()
        block = ring_row(place + way * far, rows)
        terms = []
        for side in ((way,) if far else (1, -1)):
            if (side, sub, far + 1) in where:
                term = where[side, sub, far + 1]
                sends[term].wait_recv()
                terms.append(term)

        @pl.loop(0, quarter // strip)
        def _(step):
            at = pl.multiple_of(step * strip, strip)
            mine = pl.ds(pl.multiple_of(start_of(core, sub) + at, strip), strip)
            value = x_ref[block, mine, :].astype(jnp.float32)
            value = value + mate_buf[index, pl.ds(at, strip), :].astype(jnp.float32)
            for term in terms:
                value = value + got[term, pl.ds(at, strip), :].astype(jnp.float32)
            store(at, value)

    for index, way, sub, far in reversed(lanes):

        def keep(at, value, index=index):
            made[index, pl.ds(at, strip), :] = value.astype(jnp.bfloat16)

        total(index, way, sub, far, keep)
        copy = remote(
            made.at[index], got.at[index], ring_s.at[index], ring_r.at[index],
            {"row": ring_row(place + way, rows)},
        )
        copy.start()
        sends[index] = copy
    for index, way, sub, far in wanted[-2:]:

        def split(at, value, sub=sub):
            for piece in range(cols):
                last[piece, pl.ds(sub * quarter + at, strip), :] = value[
                    :, piece * part : (piece + 1) * part
                ].astype(jnp.bfloat16)

        total(index, way, sub, far, split)
    finals = []
    for step in range(1, cols):
        target = (col + step) % cols
        copy = remote(
            last.at[target], parts.at[col], col_s.at[step - 1], col_r.at[step - 1], {"col": target}
        )
        copy.start()
        finals.append(copy)
    parts[col] = last[col]
    for copy in finals:
        copy.wait()
    for half in range(2):
        value = parts[half].astype(jnp.float32)
        for other in range(half + 2, cols, 2):
            value = value + parts[other].astype(jnp.float32)
        out_ref[half * 2 * quarter : (half + 1) * 2 * quarter, :] = value
    for copy in pairs.values():
        copy.wait_send()
    for copy in sends.values():
        copy.wait_send()


def reduce(x):
    rows, cols = lax.axis_size("row"), lax.axis_size("col")
    tok, dim = x.shape[1:]
    count = len(lanes_of(rows))
    dma = pltpu.SemaphoreType.DMA
    vmem = lambda *shape: pltpu.VMEM(shape, jnp.bfloat16)
    return pl.pallas_call(
        functools.partial(reduce_kernel, rows, cols),
        out_shape=jax.ShapeDtypeStruct((tok, dim // cols), jnp.float32),
        in_specs=[pl.BlockSpec(memory_space=pltpu.VMEM)],
        out_specs=pl.BlockSpec(memory_space=pltpu.VMEM),
        scratch_shapes=[
            vmem(count + 2, tok // 4, dim), vmem(count, tok // 4, dim), vmem(count, tok // 4, dim),
            vmem(cols, tok // 2, dim // cols), vmem(cols, tok // 2, dim // cols),
            dma((count + 2,)), dma((count + 2,)), dma((count,)), dma((count,)),
            dma((cols - 1,)), dma((cols - 1,)),
        ],
        compiler_params=pltpu.CompilerParams(
            collective_id=1, has_side_effects=True, vmem_limit_bytes=60 * 1024 * 1024
        ),
        name="reduce",
    )(x)


def local(
    tokens, moe_gain, route_ids, route_weight, w_gate, w_up, w_down, next_gain, next_gate, next_ids
):
    rows = lax.axis_size("row")
    cols = lax.axis_size("col")
    tok, dim = tokens.shape
    experts = w_gate.shape[0]
    part = dim // cols
    col = lax.axis_index("col")
    row = lax.axis_index("row")
    floats = tokens.astype(jnp.float32)
    inverse = lax.rsqrt(jnp.mean(floats * floats, axis=-1, keepdims=True) + 1e-05)
    normed = (floats * inverse * moe_gain.astype(jnp.float32)).astype(jnp.bfloat16)
    gated_in = (floats * inverse * next_gain.astype(jnp.float32)).astype(jnp.bfloat16)

    info = jnp.concatenate([route_ids.astype(jnp.float32), route_weight], axis=1)
    everyone, info = gather(normed, info.T)
    info = jnp.swapaxes(info, 1, 2)
    mine = (row * experts + jnp.arange(experts, dtype=jnp.int32)).astype(jnp.float32)
    hit = info[:, :, :TOP, None] == mine
    mask = jnp.any(hit, axis=2)
    share = jnp.sum(jnp.where(hit, info[:, :, TOP:, None], 0.0), axis=2)
    lower = jnp.arange(tok)[None, :] < jnp.arange(tok)[:, None]
    place = jnp.einsum(
        "ut,stj->suj",
        lower.astype(jnp.bfloat16),
        mask.astype(jnp.bfloat16),
        preferred_element_type=jnp.float32,
    )
    place = jnp.where(mask, place, -1.0)
    pick = (
        jnp.swapaxes(place, 1, 2)[:, :, None, :]
        == jnp.arange(CAP, dtype=jnp.float32)[None, None, :, None]
    )
    weight = jnp.sum(jnp.where(pick, jnp.swapaxes(share, 1, 2)[:, :, None, :], 0.0), axis=3)
    onehot = pick.reshape(rows, experts * CAP, tok).astype(jnp.bfloat16)

    chosen = jnp.einsum("snt,std->snd", onehot, everyone, preferred_element_type=jnp.float32)
    chosen = chosen.astype(jnp.bfloat16).reshape(rows, experts, CAP, dim)
    chosen = jnp.swapaxes(chosen, 0, 1).reshape(experts, rows * CAP, dim)

    logits = jnp.dot(gated_in, next_gate, preferred_element_type=jnp.float32)
    width = next_gate.shape[1]
    index = next_ids - col * width
    owned = index[:, :, None] == jnp.arange(width, dtype=jnp.int32)[None, None, :]
    picked = jnp.sum(jnp.where(owned, logits[:, None, :], 0.0), axis=-1)
    high = jnp.max(logits, axis=-1, keepdims=True)
    total = jnp.sum(jnp.exp(logits - high), axis=-1, keepdims=True)
    stats = lax.all_gather(jnp.concatenate([high, total, picked], axis=1), "col")
    highest = jnp.max(stats[:, :, 0], axis=0)
    sums = jnp.sum(stats[:, :, 1] * jnp.exp(stats[:, :, 0] - highest), axis=0)
    next_logprob = (
        jnp.sum(stats[:, :, 2:], axis=0) - highest[:, None] - jnp.log(sums)[:, None]
    )

    gate = jnp.einsum("jmd,jdf->jmf", chosen, w_gate, preferred_element_type=jnp.float32)
    upward = jnp.einsum("jmd,jdf->jmf", chosen, w_up, preferred_element_type=jnp.float32)
    hidden = (jax.nn.silu(gate) * upward).astype(jnp.bfloat16)
    out = jnp.einsum("jmf,jfd->jmd", hidden, w_down, preferred_element_type=jnp.float32)
    scale = jnp.swapaxes(weight, 0, 1).reshape(experts, rows * CAP, 1)
    out = (out * scale).astype(jnp.bfloat16).reshape(experts, rows, CAP, dim)
    out = jnp.swapaxes(out, 0, 1).reshape(rows, experts * CAP, dim)
    mixed = jnp.einsum("snt,snd->std", onehot, out, preferred_element_type=jnp.float32)
    mixed = mixed.astype(jnp.bfloat16)
    mixed = reduce(mixed)
    residual = lax.dynamic_slice_in_dim(floats, col * part, part, 1)
    return ((residual + mixed).astype(jnp.bfloat16), next_logprob)


def solution(mesh):
    placed = (
        P("row", None),
        P(),
        P("row", None),
        P("row", None),
        P("row", None, "col"),
        P("row", None, "col"),
        P("row", "col", None),
        P(),
        P(None, "col"),
        P("row", None),
    )
    return jax.shard_map(
        local,
        mesh=mesh,
        in_specs=placed,
        out_specs=(P("row", "col"), P("row", None)),
        check_vma=False,
    )
```

```python
import functools

import jax
import jax.numpy as jnp
from jax import lax
from jax.experimental import pallas as pl
from jax.experimental.pallas import tpu as pltpu
from jax.sharding import PartitionSpec as P

TOP = 4
CAP = 24


MESH = pl.DeviceIdType.MESH


def ring_place(row, rows):
    return row // 2 + (row % 2) * (rows - 1 - 2 * (row // 2))


def ring_row(place, rows):
    place = (place + 2 * rows) % rows
    far = place // (rows // 2)
    return (1 - far) * 2 * place + far * (2 * (rows - 1 - place) + 1)


def lanes_of(rows):
    half = rows // 2
    found = []
    for distance in range(1, half + 1):
        for way in (0, 1):
            for sub in (0, 1):
                if distance < half or way == sub:
                    found.append((len(found), 1 - 2 * way, sub, distance))
    return found


def remote(src, dst, send, recv, target):
    return pltpu.make_async_remote_copy(
        src_ref=src, dst_ref=dst, send_sem=send, recv_sem=recv, device_id=target, device_id_type=MESH
    )


def greet(rows, cols, all_cols):
    row, col = lax.axis_index("row"), lax.axis_index("col")
    barrier = pltpu.get_barrier_semaphore()
    for step in range(1, rows):
        pl.semaphore_signal(
            barrier, inc=1, device_id={"row": (row + step) % rows}, device_id_type=MESH
        )
    others = range(1, cols) if all_cols else ()
    for step in others:
        pl.semaphore_signal(
            barrier, inc=1, device_id={"col": (col + step) % cols}, device_id_type=MESH
        )
    pl.semaphore_wait(barrier, rows - 1 + len(others))


def gather_kernel(
    rows, cols, x_ref, info_ref, out_ref, all_ref, ring_s, ring_r, pair_s, pair_r, info_s, info_r, own_s
):
    row, col = lax.axis_index("row"), lax.axis_index("col")
    core = col % 2
    mate = {"col": col + 1 - 2 * core}
    place = ring_place(row, rows)
    tok = x_ref.shape[0]
    quarter = tok // 4
    greet(rows, cols, True)
    infos = []
    for step in range(1, rows):
        copy = remote(
            info_ref, all_ref.at[row], info_s.at[step - 1], info_r.at[step - 1],
            {"row": (row + step) % rows},
        )
        copy.start()
        infos.append(copy)
    own = pltpu.make_async_copy(x_ref, out_ref.at[row], own_s)

    def span(sub):
        return pl.ds(pl.multiple_of(core * 2 * quarter, quarter) + sub * quarter, quarter)

    lanes = lanes_of(rows)
    where = {(way, sub, far): index for index, way, sub, far in lanes}
    sends = {}

    def send(way, sub, far):
        index = where[way, sub, far]
        block = ring_row(place - way * (far - 1), rows)
        src = x_ref.at[span(sub)] if far == 1 else out_ref.at[block, span(sub)]
        copy = remote(
            src, out_ref.at[block, span(sub)], ring_s.at[index], ring_r.at[index],
            {"row": ring_row(place + way, rows)},
        )
        copy.start()
        sends[index] = copy

    for index, way, sub, far in lanes:
        if far == 1:
            send(way, sub, far)
    own.start()
    pairs = []
    for index, way, sub, far in lanes:
        sends[index].wait_recv()
        if (way, sub, far + 1) in where:
            send(way, sub, far + 1)
        block = ring_row(place - way * far, rows)
        piece = out_ref.at[block, span(sub)]
        copy = remote(piece, piece, pair_s.at[index], pair_r.at[index], mate)
        copy.start()
        pairs.append(copy)
    all_ref[row] = info_ref[...]
    for copy in infos:
        copy.wait()
    own.wait()
    for index, *_ in lanes:
        sends[index].wait_send()
    for copy in pairs:
        copy.wait()


def gather(x, info):
    rows, cols = lax.axis_size("row"), lax.axis_size("col")
    count = len(lanes_of(rows))
    dma = pltpu.SemaphoreType.DMA
    return pl.pallas_call(
        functools.partial(gather_kernel, rows, cols),
        out_shape=(
            jax.ShapeDtypeStruct((rows,) + x.shape, x.dtype),
            jax.ShapeDtypeStruct((rows,) + info.shape, info.dtype),
        ),
        in_specs=[pl.BlockSpec(memory_space=pltpu.VMEM)] * 2,
        out_specs=(pl.BlockSpec(memory_space=pl.ANY), pl.BlockSpec(memory_space=pltpu.VMEM)),
        scratch_shapes=[
            dma((count,)), dma((count,)), dma((count,)), dma((count,)),
            dma((rows - 1,)), dma((rows - 1,)), dma(()),
        ],
        compiler_params=pltpu.CompilerParams(collective_id=0, has_side_effects=True),
        name="gather",
    )(x, info)


def reduce_kernel(
    rows, cols, x_ref, out_ref, mate_buf, got, made, last, parts,
    pair_s, pair_r, ring_s, ring_r, col_s, col_r,
):
    row, col = lax.axis_index("row"), lax.axis_index("col")
    core = col % 2
    place = ring_place(row, rows)
    tok, dim = x_ref.shape[1:]
    quarter = tok // 4
    part = dim // cols
    strip = 16
    greet(rows, cols, True)
    lanes = lanes_of(rows)
    where = {(way, sub, far): index for index, way, sub, far in lanes}
    wanted = list(reversed(lanes)) + [(len(lanes), 1, 0, 0), (len(lanes) + 1, 1, 1, 0)]

    def start_of(owner, sub):
        return pl.multiple_of(owner * 2 * quarter, quarter) + sub * quarter

    pairs = {}
    for index, way, sub, far in wanted:
        block = ring_row(place + way * far, rows)
        copy = remote(
            x_ref.at[block, pl.ds(start_of(1 - core, sub), quarter)], mate_buf.at[index],
            pair_s.at[index], pair_r.at[index], {"col": col + 1 - 2 * core},
        )
        copy.start()
        pairs[index] = copy
    sends = {}

    def total(index, way, sub, far, store):
        pairs[index].wait_recv()
        block = ring_row(place + way * far, rows)
        terms = []
        for side in ((way,) if far else (1, -1)):
            if (side, sub, far + 1) in where:
                term = where[side, sub, far + 1]
                sends[term].wait_recv()
                terms.append(term)

        @pl.loop(0, quarter // strip)
        def _(step):
            at = pl.multiple_of(step * strip, strip)
            mine = pl.ds(pl.multiple_of(start_of(core, sub) + at, strip), strip)
            value = x_ref[block, mine, :].astype(jnp.float32)
            value = value + mate_buf[index, pl.ds(at, strip), :].astype(jnp.float32)
            for term in terms:
                value = value + got[term, pl.ds(at, strip), :].astype(jnp.float32)
            store(at, value)

    for index, way, sub, far in reversed(lanes):

        def keep(at, value, index=index):
            made[index, pl.ds(at, strip), :] = value.astype(jnp.bfloat16)

        total(index, way, sub, far, keep)
        copy = remote(
            made.at[index], got.at[index], ring_s.at[index], ring_r.at[index],
            {"row": ring_row(place + way, rows)},
        )
        copy.start()
        sends[index] = copy
    for index, way, sub, far in wanted[-2:]:

        def split(at, value, sub=sub):
            for piece in range(cols):
                last[piece, pl.ds(sub * quarter + at, strip), :] = value[
                    :, piece * part : (piece + 1) * part
                ].astype(jnp.bfloat16)

        total(index, way, sub, far, split)
    finals = []
    for step in range(1, cols):
        target = (col + step) % cols
        copy = remote(
            last.at[target], parts.at[col], col_s.at[step - 1], col_r.at[step - 1], {"col": target}
        )
        copy.start()
        finals.append(copy)
    parts[col] = last[col]
    for copy in finals:
        copy.wait()
    for half in range(2):
        value = parts[half].astype(jnp.float32)
        for other in range(half + 2, cols, 2):
            value = value + parts[other].astype(jnp.float32)
        out_ref[half * 2 * quarter : (half + 1) * 2 * quarter, :] = value
    for copy in pairs.values():
        copy.wait_send()
    for copy in sends.values():
        copy.wait_send()


def reduce(x):
    rows, cols = lax.axis_size("row"), lax.axis_size("col")
    tok, dim = x.shape[1:]
    count = len(lanes_of(rows))
    dma = pltpu.SemaphoreType.DMA
    vmem = lambda *shape: pltpu.VMEM(shape, jnp.bfloat16)
    return pl.pallas_call(
        functools.partial(reduce_kernel, rows, cols),
        out_shape=jax.ShapeDtypeStruct((tok, dim // cols), jnp.float32),
        in_specs=[pl.BlockSpec(memory_space=pltpu.VMEM)],
        out_specs=pl.BlockSpec(memory_space=pltpu.VMEM),
        scratch_shapes=[
            vmem(count + 2, tok // 4, dim), vmem(count, tok // 4, dim), vmem(count, tok // 4, dim),
            vmem(cols, tok // 2, dim // cols), vmem(cols, tok // 2, dim // cols),
            dma((count + 2,)), dma((count + 2,)), dma((count,)), dma((count,)),
            dma((cols - 1,)), dma((cols - 1,)),
        ],
        compiler_params=pltpu.CompilerParams(
            collective_id=1, has_side_effects=True, vmem_limit_bytes=60 * 1024 * 1024
        ),
        name="reduce",
    )(x)


def place_kernel(pick_ref, x_ref, out_ref):
    value = jnp.dot(pick_ref[0], x_ref[0], preferred_element_type=jnp.float32)
    experts, _, slots, _ = out_ref.shape
    for expert in range(experts):
        out_ref[expert, 0] = value[expert * slots : (expert + 1) * slots].astype(jnp.bfloat16)


def place_tokens(pick, x, experts):
    rows, count, tok = pick.shape
    dim = x.shape[2]
    slots = count // experts
    return pl.pallas_call(
        place_kernel,
        grid=(rows,),
        out_shape=jax.ShapeDtypeStruct((experts, rows, slots, dim), jnp.bfloat16),
        in_specs=[
            pl.BlockSpec((1, count, tok), lambda s: (s, 0, 0)),
            pl.BlockSpec((1, tok, dim), lambda s: (s, 0, 0)),
        ],
        out_specs=pl.BlockSpec((experts, 1, slots, dim), lambda s: (0, s, 0, 0)),
        name="place",
    )(pick, x)


def join_kernel(back_ref, x_ref, out_ref, flat):
    experts, _, slots, _ = x_ref.shape
    for expert in range(experts):
        flat[expert * slots : (expert + 1) * slots, :] = x_ref[expert, 0].astype(jnp.float32)
    value = jnp.dot(
        back_ref[0], flat[...].astype(jnp.bfloat16), preferred_element_type=jnp.float32
    )
    out_ref[0] = value.astype(jnp.bfloat16)


def join_tokens(back, x):
    rows, tok, count = back.shape
    experts, _, slots, dim = x.shape
    return pl.pallas_call(
        join_kernel,
        grid=(rows,),
        out_shape=jax.ShapeDtypeStruct((rows, tok, dim), jnp.bfloat16),
        in_specs=[
            pl.BlockSpec((1, tok, count), lambda s: (s, 0, 0)),
            pl.BlockSpec((experts, 1, slots, dim), lambda s: (0, s, 0, 0)),
        ],
        out_specs=pl.BlockSpec((1, tok, dim), lambda s: (s, 0, 0)),
        scratch_shapes=[pltpu.VMEM((count, dim), jnp.float32)],
        name="join",
    )(back, x)


def local(
    tokens, moe_gain, route_ids, route_weight, w_gate, w_up, w_down, next_gain, next_gate, next_ids
):
    rows = lax.axis_size("row")
    cols = lax.axis_size("col")
    tok, dim = tokens.shape
    experts = w_gate.shape[0]
    part = dim // cols
    col = lax.axis_index("col")
    row = lax.axis_index("row")
    floats = tokens.astype(jnp.float32)
    inverse = lax.rsqrt(jnp.mean(floats * floats, axis=-1, keepdims=True) + 1e-05)
    normed = (floats * inverse * moe_gain.astype(jnp.float32)).astype(jnp.bfloat16)
    gated_in = (floats * inverse * next_gain.astype(jnp.float32)).astype(jnp.bfloat16)

    info = jnp.concatenate([route_ids.astype(jnp.float32), route_weight], axis=1)
    everyone, info = gather(normed, info.T)
    info = jnp.swapaxes(info, 1, 2)
    mine = (row * experts + jnp.arange(experts, dtype=jnp.int32)).astype(jnp.float32)
    hit = info[:, :, :TOP, None] == mine
    mask = jnp.any(hit, axis=2)
    share = jnp.sum(jnp.where(hit, info[:, :, TOP:, None], 0.0), axis=2)
    lower = jnp.arange(tok)[None, :] < jnp.arange(tok)[:, None]
    place = jnp.einsum(
        "ut,stj->suj",
        lower.astype(jnp.bfloat16),
        mask.astype(jnp.bfloat16),
        preferred_element_type=jnp.float32,
    )
    place = jnp.where(mask, place, -1.0)
    pick = (
        jnp.swapaxes(place, 1, 2)[:, :, None, :]
        == jnp.arange(CAP, dtype=jnp.float32)[None, None, :, None]
    )
    weight = jnp.sum(jnp.where(pick, jnp.swapaxes(share, 1, 2)[:, :, None, :], 0.0), axis=3)
    onehot = pick.reshape(rows, experts * CAP, tok).astype(jnp.bfloat16)

    chosen = place_tokens(onehot, everyone, experts).reshape(experts, rows * CAP, dim)

    logits = jnp.dot(gated_in, next_gate, preferred_element_type=jnp.float32)
    width = next_gate.shape[1]
    index = next_ids - col * width
    owned = index[:, :, None] == jnp.arange(width, dtype=jnp.int32)[None, None, :]
    picked = jnp.sum(jnp.where(owned, logits[:, None, :], 0.0), axis=-1)
    high = jnp.max(logits, axis=-1, keepdims=True)
    total = jnp.sum(jnp.exp(logits - high), axis=-1, keepdims=True)
    stats = lax.all_gather(jnp.concatenate([high, total, picked], axis=1), "col")
    highest = jnp.max(stats[:, :, 0], axis=0)
    sums = jnp.sum(stats[:, :, 1] * jnp.exp(stats[:, :, 0] - highest), axis=0)
    next_logprob = (
        jnp.sum(stats[:, :, 2:], axis=0) - highest[:, None] - jnp.log(sums)[:, None]
    )

    gate = jnp.einsum("jmd,jdf->jmf", chosen, w_gate, preferred_element_type=jnp.float32)
    upward = jnp.einsum("jmd,jdf->jmf", chosen, w_up, preferred_element_type=jnp.float32)
    hidden = (jax.nn.silu(gate) * upward).astype(jnp.bfloat16)
    out = jnp.einsum("jmf,jfd->jmd", hidden, w_down, preferred_element_type=jnp.float32)
    scale = jnp.swapaxes(weight, 0, 1).reshape(experts, rows * CAP, 1)
    out = (out * scale).astype(jnp.bfloat16).reshape(experts, rows, CAP, dim)
    mixed = join_tokens(jnp.swapaxes(onehot, 1, 2), out)
    mixed = reduce(mixed)
    residual = lax.dynamic_slice_in_dim(floats, col * part, part, 1)
    return ((residual + mixed).astype(jnp.bfloat16), next_logprob)


def solution(mesh):
    placed = (
        P("row", None),
        P(),
        P("row", None),
        P("row", None),
        P("row", None, "col"),
        P("row", None, "col"),
        P("row", "col", None),
        P(),
        P(None, "col"),
        P("row", None),
    )
    return jax.shard_map(
        local,
        mesh=mesh,
        in_specs=placed,
        out_specs=(P("row", "col"), P("row", None)),
        check_vma=False,
    )
```
